32 devices in a mesh: layer: 4 (over z), row: 4 (over x, core), col: 2 (over y).
Axes of the slice: x: 2, y: 2, z: 4, core: 2. Of those that a mesh axis runs over, the one named last changes fastest.
Arguments:
- rhs_low: bfloat16 [4, 2, 2, 384, 512], P('layer', None, 'col'), may hold values from -6 to 6
- inv_low: bfloat16 [4, 2, 2, 384, 384], P('layer', None, 'col'), as said below
- blocks: bfloat16 [4, 4, 2, 2, 4, 384, 384], P('layer', 'row', 'col'), may hold values from -0.02734375 to 0.02734375
- targets: int32 [4, 4, 2, 2, 4], P('layer', 'row', 'col'), may hold values from 1 to 5, as said below
- rhs_anc: bfloat16 [16, 384, 512], P('row', None, ('layer', 'col')), may hold values from -6 to 6
- inv_anc: bfloat16 [16, 384, 384], P('row'), as said below
Outputs:
- solution_low: bfloat16 [4, 2, 2, 384, 512], P('layer', None, 'col', None, 'row')
- solution_anc: float32 [16, 384, 512], P('row', None, ('layer', 'col'))
The draws below stay inside these ranges and needn't reach their ends.
Inputs may be any that keep to these rules, and one draw needn't show every extreme that they name: For each g, r, c, l the 4 values targets[g, r, c, l, :] are distinct. A value t < 2 is greater than l; a value t >= 2 names ancestor r * 4 + t - 2. `inv_low`: each block is lower triangular. `inv_anc`: each block is lower triangular.
All inputs are finite; a program needn't handle non-finite values.
Results may differ from the reference program's by a relative error of at most 0.011.
Values may be sent and summed in bfloat16 or wider, within the bound.
A program may use at most 64 MiB of HBM per device.

```python
import jax
import jax.numpy as jnp
from jax import lax

W = 384
R = 512
LEVELS = 2
BPR = 4
LAYERS = 4
GRID_ROWS = 4
GRID_COLS = 2
ANC_ROW = 4
ANC = 16


def lower_block(key, count):
    first, second = jax.random.split(key)
    below = jax.random.normal(second, (count, W, W), jnp.float32) * 0.8 / jnp.sqrt(1.0 * W)
    middle = jax.random.uniform(first, (count, W), jnp.float32, 0.6, 1.4)
    return jnp.tril(below, -1) + middle[:, :, None] * jnp.eye(W, dtype=jnp.float32)[None]


def draw_inv_low(key, part):
    matrix = lower_block(jax.random.fold_in(key, 5), LAYERS * LEVELS * GRID_COLS)
    return matrix.reshape(LAYERS, LEVELS, GRID_COLS, W, W).astype(jnp.bfloat16)


def draw_inv_anc(key, part):
    matrix = lower_block(jax.random.fold_in(key, 11), ANC)
    return matrix.astype(jnp.bfloat16)


def draw_targets(key, part):
    key = jax.random.fold_in(key, 3)
    total_options = LEVELS + ANC_ROW
    full_shape = (LAYERS, GRID_ROWS, GRID_COLS, LEVELS, total_options)
    option = jnp.arange(total_options, dtype=jnp.int32).reshape(1, 1, 1, 1, -1)
    source = jnp.arange(LEVELS, dtype=jnp.int32).reshape(1, 1, 1, -1, 1)
    holder = jnp.arange(GRID_ROWS, dtype=jnp.int32).reshape(1, -1, 1, 1, 1)
    inside = (option > source) & (option < LEVELS) & (jnp.mod(holder - option, GRID_ROWS) < GRID_COLS)
    allowed = inside | (option >= LEVELS)
    scores = jax.random.randint(key, full_shape, 0, 1 << 20, dtype=jnp.int32) * total_options + option
    scores = jnp.where(allowed, scores, -1)
    picked = lax.top_k(scores, BPR)[1]
    return picked.astype(jnp.int32)


def steps_of(own_key, extent, cuts, smallest, largest):
    loudness, own = 1.0, jax.random.fold_in(own_key, 6)
    for position, shards_of in cuts:
        heights = jnp.exp(jax.random.uniform(jax.random.fold_in(own, position), (shards_of,), jnp.float32, smallest / len(cuts), largest / len(cuts)))
        loudness = loudness * jnp.repeat(heights, extent[position] // shards_of).reshape([-1 if axis == position else 1 for axis in range(len(extent))])
    return loudness


def centred(key, dims, spread, bound, cuts=(), held_as=jnp.bfloat16):
    array = jax.random.normal(key, dims, jnp.float32) * spread
    if len(cuts) > 0:
        array = steps_of(key, dims, cuts, -0.22, 0.18) * array
    return jnp.clip(array, min=-bound, max=bound).astype(held_as)


def setup_inputs(seed: int = 0) -> dict:
    keys = jax.random.split(jax.random.key(seed), 7)
    return {
        "rhs_low": centred(keys[0], (LAYERS, LEVELS, GRID_COLS, W, R), 1.0, 6.0, ((0, 4), (2, 2))),
        "inv_low": draw_inv_low(jax.random.fold_in(keys[6], 71), 0),
        "blocks": centred(keys[2], (LAYERS, GRID_ROWS, GRID_COLS, LEVELS, BPR, W, W), (128 * W) ** -0.5, 0.02734375, ((0, 4), (1, 4), (2, 2))),
        "targets": draw_targets(jax.random.fold_in(keys[6], 71), 0),
        "rhs_anc": centred(keys[4], (ANC, W, R), 1.0, 6.0, ((0, 4), (2, 8))),
        "inv_anc": draw_inv_anc(jax.random.fold_in(keys[6], 71), 0),
    }


def layer_solve(rhs_layer, inv_layer, block_layer, target_layer):
    collected = jnp.zeros((GRID_ROWS, LEVELS + ANC_ROW, W, R), jnp.float32)
    row_ids = jnp.broadcast_to(jnp.arange(GRID_ROWS, dtype=jnp.int32)[:, None, None], (GRID_ROWS, GRID_COLS, BPR))
    solved = []
    for current in range(LEVELS):
        owners = (current + jnp.arange(GRID_COLS, dtype=jnp.int32)) % GRID_ROWS
        partial_value = collected[owners, current]
        residual = (rhs_layer[current].astype(jnp.float32) - partial_value).astype(jnp.bfloat16)
        answer = jnp.einsum("cwv,cvk->cwk", inv_layer[current].astype(jnp.float32), residual.astype(jnp.float32)).astype(jnp.bfloat16)
        solved.append(answer)
        product = jnp.einsum("rcswv,cvk->rcswk", block_layer[:, :, current].astype(jnp.float32), answer.astype(jnp.float32))
        collected = collected.at[row_ids, target_layer[:, :, current]].add(product)
    return jnp.stack(solved, 0), collected[:, LEVELS:]


def reference(rhs_low, inv_low, blocks, targets, rhs_anc, inv_anc):
    def one_layer(members):
        return layer_solve(members[0], members[1], members[2], members[3])

    solution_low, ancestor_parts = lax.map(one_layer, (rhs_low, inv_low, blocks, targets))
    ancestor_partial = jnp.sum(ancestor_parts, axis=0).reshape(ANC, W, R)
    residual = (rhs_anc.astype(jnp.float32) - ancestor_partial).astype(jnp.bfloat16)
    solution_anc = jnp.einsum("awv,avk->awk", inv_anc.astype(jnp.float32), residual.astype(jnp.float32))
    return solution_low, solution_anc
```

```python
import functools

import jax
import jax.numpy as jnp
from jax import lax
from jax.experimental import pallas as pl
from jax.experimental.pallas import tpu as pltpu
from jax.sharding import PartitionSpec as P

MESH = pl.DeviceIdType.MESH
F32 = jnp.float32
BF16 = jnp.bfloat16


def dot_t(left, right):
    return lax.dot_general(left, right, (((1,), (1,)), ((), ())), preferred_element_type=F32)


def kernel(
    sizes,
    targets,
    rhs_hbm,
    inv_hbm,
    blocks_hbm,
    rhs_anc_hbm,
    inv_anc_hbm,
    low_out,
    anc_out,
    rhs,
    inv,
    blocks0,
    blocks1,
    rhs_anc,
    inv_anc,
    low,
    x0,
    x1,
    part,
    part_in,
    right,
    base,
    packed,
    y_in,
    z_out,
    z_in,
    load_sem,
    out_sem,
    p_send,
    p_recv,
    x_send,
    x_recv,
    y_send,
    y_recv,
    z_send,
    z_recv,
):
    layers, rows, cols = sizes
    layer, row, col = (lax.axis_index(a) for a in ("layer", "row", "col"))
    slots = blocks0.shape[0]
    anc_row, narrow, width = rhs_anc.shape
    share = x1.shape[1]

    def ordered(k):
        return (row // 2 * 2 + k // 2 * 2) % rows + (row + k) % 2

    barrier = pltpu.get_barrier_semaphore()
    for dr in range(rows):
        for dc in range(cols):
            if dr or dc:
                pl.semaphore_signal(
                    barrier,
                    inc=1,
                    device_id={"row": (row + dr) % rows, "col": (col + dc) % cols},
                    device_id_type=MESH,
                )
    for dl in range(1, layers):
        pl.semaphore_signal(
            barrier, inc=1, device_id={"layer": (layer + dl) % layers}, device_id_type=MESH
        )

    loads = [
        pltpu.make_async_copy(inv_hbm.at[0], inv.at[0], load_sem.at[0]),
        pltpu.make_async_copy(rhs_hbm.at[0], rhs.at[0], load_sem.at[1]),
        pltpu.make_async_copy(blocks_hbm.at[0], blocks0, load_sem.at[2]),
        pltpu.make_async_copy(inv_hbm.at[1], inv.at[1], load_sem.at[3]),
        pltpu.make_async_copy(rhs_hbm.at[1], rhs.at[1], load_sem.at[4]),
        pltpu.make_async_copy(blocks_hbm.at[1], blocks1, load_sem.at[5]),
        pltpu.make_async_copy(inv_anc_hbm, inv_anc, load_sem.at[6]),
        pltpu.make_async_copy(rhs_anc_hbm, rhs_anc, load_sem.at[7]),
    ]
    for load in loads:
        load.start()

    def listed(level, target):
        index, found = jnp.int32(0), jnp.int32(0)
        for s in range(slots):
            hit = (targets[level, s] == target).astype(jnp.int32)
            index = index + hit * s
            found = found + hit
        return (blocks0, blocks1)[level][index], found.astype(F32)

    def span(j):
        return pl.ds(pl.multiple_of(j * share, share), share)

    loads[0].wait()
    loads[1].wait()
    first = jnp.dot(inv[0], rhs[0], preferred_element_type=F32)
    x0[...] = first.T.astype(BF16)

    loads[2].wait()
    goal = (row + rows - 1) % rows
    active = goal < cols
    owner = (1 + col) % rows

    def p_copy(k):
        j = ordered(k)
        return pltpu.make_async_remote_copy(
            src_ref=part.at[j],
            dst_ref=part_in.at[col],
            send_sem=p_send.at[k],
            recv_sem=p_recv.at[col],
            device_id={"row": j, "col": goal},
            device_id_type=MESH,
        )

    pl.semaphore_wait(barrier, rows * cols - 1 + layers - 1)

    @pl.when(active)
    def _():
        block, found = listed(0, 1)
        for k in range(rows):
            j = ordered(k)
            value = dot_t(x0[span(j), :], block) * found
            part[j] = value.astype(BF16)
            if k == 0:

                @pl.when(goal != col)
                def _():
                    p_copy(0).start()

                @pl.when(goal == col)
                def _():
                    part_in[col] = part[row]

            else:
                p_copy(k).start()

    for j in range(rows):

        @pl.when(row == j)
        def _():
            low[0] = x0[j * share : (j + 1) * share, :].astype(F32).T.astype(BF16)

    low0 = pltpu.make_async_copy(low.at[0], low_out.at[0], out_sem.at[0])
    low0.start()

    for a in range(anc_row):
        block, found = listed(0, a + 2)
        base[:, a * width : (a + 1) * width] = dot_t(x0[...], block) * found

    loads[3].wait()
    loads[4].wait()
    for j in range(rows):

        @pl.when(row == j)
        def _():
            right[...] = rhs[1, :, j * share : (j + 1) * share].astype(F32).T

    for cc in range(cols):

        @pl.when(jnp.logical_or(col != cc, row != owner))
        def _():
            pltpu.make_async_remote_copy(
                src_ref=part.at[0],
                dst_ref=part_in.at[cc],
                send_sem=p_send.at[0],
                recv_sem=p_recv.at[cc],
                device_id={"row": row, "col": col},
                device_id_type=MESH,
            ).wait_recv()

    total = part_in[0].astype(F32)
    for cc in range(1, cols):
        total = total + part_in[cc].astype(F32)
    residual = (right[...] - total).astype(BF16)
    x1[row] = dot_t(residual, inv[1]).astype(BF16)

    def x_copy(k, slot):
        return pltpu.make_async_remote_copy(
            src_ref=x1.at[slot],
            dst_ref=x1.at[slot],
            send_sem=x_send.at[k],
            recv_sem=x_recv.at[slot],
            device_id={"row": ordered(k)},
            device_id_type=MESH,
        )

    for k in range(1, rows):
        x_copy(k, row).start()

    def y_copy(d, j):
        cc = (col + d) % cols
        return pltpu.make_async_remote_copy(
            src_ref=packed.at[cc, j],
            dst_ref=y_in.at[d - 1, j],
            send_sem=y_send.at[d - 1, j],
            recv_sem=y_recv.at[d - 1, j],
            device_id={"col": cc},
            device_id_type=MESH,
        )

    loads[5].wait()
    for k in range(rows):
        j = ordered(k)
        if k:
            x_copy(k, j).wait_recv()
        for a in range(anc_row):
            block, found = listed(1, a + 2)
            at = slice(a * width, (a + 1) * width)
            value = base[span(j), at] + dot_t(x1[j], block) * found
            value = value.astype(BF16)
            for cc in range(cols):
                packed[cc, j, :, at] = value[cc * narrow : (cc + 1) * narrow]
        for d in range(1, cols):
            y_copy(d, j).start()
        if k == 0:
            low[1] = x1[row].astype(F32).T.astype(BF16)
            low1 = pltpu.make_async_copy(low.at[1], low_out.at[1], out_sem.at[1])
            low1.start()

    def z_copy(j):
        return pltpu.make_async_remote_copy(
            src_ref=z_out.at[j],
            dst_ref=z_in.at[layer],
            send_sem=z_send.at[j],
            recv_sem=z_recv.at[layer],
            device_id={"layer": j},
            device_id_type=MESH,
        )

    for k in range(rows):
        j = ordered(k)
        merged = packed[col, j].astype(F32)
        for d in range(1, cols):
            y_copy(d, j).wait_recv()
            merged = merged + y_in[d - 1, j].astype(F32)

        @pl.when(j != layer)
        def _():
            z_out[j] = merged.astype(BF16)
            z_copy(j).start()

        @pl.when(j == layer)
        def _():
            z_in[layer] = merged.astype(BF16)

    loads[6].wait()
    loads[7].wait()
    for s in range(layers):

        @pl.when(layer != s)
        def _():
            pltpu.make_async_remote_copy(
                src_ref=z_out.at[s],
                dst_ref=z_in.at[s],
                send_sem=z_send.at[s],
                recv_sem=z_recv.at[s],
                device_id={"layer": layer},
                device_id_type=MESH,
            ).wait_recv()

    for a in range(anc_row):
        residual = rhs_anc[a].astype(F32)
        for s in range(layers):
            residual = residual - z_in[s, :, a * width : (a + 1) * width].astype(F32)
        anc_out[a] = dot_t(residual.astype(BF16), inv_anc[a])

    @pl.when(active)
    def _():
        for k in range(rows):
            if k == 0:

                @pl.when(goal != col)
                def _():
                    p_copy(0).wait_send()

            else:
                p_copy(k).wait_send()

    for k in range(1, rows):
        x_copy(k, row).wait_send()
    for k in range(rows):
        j = ordered(k)
        for d in range(1, cols):
            y_copy(d, j).wait_send()

        @pl.when(j != layer)
        def _():
            z_copy(j).wait_send()

    low0.wait()
    low1.wait()


def on_device(sizes, rhs_low, inv_low, blocks, targets, rhs_anc, inv_anc):
    layers, rows, cols = sizes
    levels, slots = blocks.shape[3], blocks.shape[4]
    width, cases = rhs_low.shape[3], rhs_low.shape[4]
    anc_row, narrow = rhs_anc.shape[0], rhs_anc.shape[2]
    share = cases // rows
    assert levels == 2 and layers == rows and cols <= rows and cols * narrow == share
    any_space = pl.BlockSpec(memory_space=pl.ANY)
    dma = pltpu.SemaphoreType.DMA
    low, anc = pl.pallas_call(
        functools.partial(kernel, sizes),
        out_shape=(
            jax.ShapeDtypeStruct((levels, width, share), BF16),
            jax.ShapeDtypeStruct((anc_row, narrow, width), F32),
        ),
        in_specs=[pl.BlockSpec(memory_space=pltpu.SMEM)] + [any_space] * 5,
        out_specs=(any_space, pl.BlockSpec(memory_space=pltpu.VMEM)),
        scratch_shapes=[
            pltpu.VMEM((levels, width, cases), BF16),
            pltpu.VMEM((levels, width, width), BF16),
            pltpu.VMEM((slots, width, width), BF16),
            pltpu.VMEM((slots, width, width), BF16),
            pltpu.VMEM((anc_row, narrow, width), BF16),
            pltpu.VMEM((anc_row, width, width), BF16),
            pltpu.VMEM((levels, width, share), BF16),
            pltpu.VMEM((cases, width), BF16),
            pltpu.VMEM((rows, share, width), BF16),
            pltpu.VMEM((rows, share, width), BF16),
            pltpu.VMEM((cols, share, width), BF16),
            pltpu.VMEM((share, width), F32),
            pltpu.VMEM((cases, anc_row * width), F32),
            pltpu.VMEM((cols, rows, narrow, anc_row * width), BF16),
            pltpu.VMEM((cols - 1, rows, narrow, anc_row * width), BF16),
            pltpu.VMEM((layers, narrow, anc_row * width), BF16),
            pltpu.VMEM((layers, narrow, anc_row * width), BF16),
            dma((8,)),
            dma((2,)),
            dma((rows,)),
            dma((cols,)),
            dma((rows,)),
            dma((rows,)),
            dma((cols - 1, rows)),
            dma((cols - 1, rows)),
            dma((layers,)),
            dma((layers,)),
        ],
        compiler_params=pltpu.CompilerParams(
            collective_id=0, has_side_effects=True, vmem_limit_bytes=56 * 1024 * 1024
        ),
    )(
        targets.reshape(levels, slots),
        rhs_low.reshape(levels, width, cases),
        inv_low.reshape(levels, width, width),
        blocks.reshape(levels, slots, width, width),
        rhs_anc.transpose(0, 2, 1),
        inv_anc,
    )
    return low[None, :, None], anc.transpose(0, 2, 1)


def solution(mesh):
    sizes = tuple(mesh.shape[a] for a in ("layer", "row", "col"))
    in_specs = (
        P("layer", None, "col", None, None),
        P("layer", None, "col", None, None),
        P("layer", "row", "col", None, None, None, None),
        P("layer", "row", "col", None, None),
        P("row", None, ("layer", "col")),
        P("row", None, None),
    )
    out_specs = (P("layer", None, "col", None, "row"), P("row", None, ("layer", "col")))
    return jax.shard_map(
        functools.partial(on_device, sizes),
        mesh=mesh,
        in_specs=in_specs,
        out_specs=out_specs,
        check_vma=False,
    )
```

```python
import functools

import jax
import jax.numpy as jnp
from jax import lax
from jax.experimental import pallas as pl
from jax.experimental.pallas import tpu as pltpu
from jax.sharding import PartitionSpec as P

MESH = pl.DeviceIdType.MESH
F32 = jnp.float32
BF16 = jnp.bfloat16


def dot_t(left, right):
    return lax.dot_general(left, right, (((1,), (1,)), ((), ())), preferred_element_type=F32)


def kernel(
    sizes,
    targets,
    rhs_hbm,
    inv_hbm,
    blocks_hbm,
    rhs_anc_hbm,
    inv_anc_hbm,
    low_out,
    anc_out,
    rhs,
    inv,
    blocks0,
    blocks1,
    rhs_anc,
    inv_anc,
    low,
    x0,
    x1,
    part,
    part_in,
    right,
    base,
    packed,
    y_in,
    z_out,
    z_in,
    load_sem,
    out_sem,
    p_send,
    p_recv,
    x_send,
    x_recv,
    y_send,
    y_recv,
    z_send,
    z_recv,
):
    layers, rows, cols = sizes
    layer, row, col = (lax.axis_index(a) for a in ("layer", "row", "col"))
    slots = blocks0.shape[0]
    anc_row, narrow, width = rhs_anc.shape
    share = x1.shape[1]

    def ordered(k):
        return (row // 2 * 2 + k // 2 * 2) % rows + (row + k) % 2

    def flag(condition):
        return condition.astype(jnp.int32)

    last = layers - 1
    relayed = flag(layer == 1) * last - flag(layer != 1)
    relayed = relayed + flag(layer == last - 1) * (0 - relayed)
    opening = row + flag(row == layer) * (ordered(1) - row)
    keys = []
    for j in range(rows):
        place = 0
        for k in range(rows):
            place = place + k * flag(ordered(k) == j)
        key = place - 16 * jnp.abs(layer - j)
        key = key + 500 * flag(relayed == j) + 5000 * flag(layer == j) - 2000 * flag(opening == j)
        keys.append(key)
    order = [0] * rows
    for j in range(rows):
        rank = 0
        for other in range(rows):
            if other != j:
                rank = rank + flag(keys[other] < keys[j])
        order = [order[k] + j * flag(rank == k) for k in range(rows)]
    swap = flag(relayed == opening) * (order[1] - order[0])
    merge_order = [order[0] + swap, order[1] - swap] + order[2:]

    barrier = pltpu.get_barrier_semaphore()
    for dr in range(rows):
        for dc in range(cols):
            if dr or dc:
                pl.semaphore_signal(
                    barrier,
                    inc=1,
                    device_id={"row": (row + dr) % rows, "col": (col + dc) % cols},
                    device_id_type=MESH,
                )
    for dl in range(1, layers):
        pl.semaphore_signal(
            barrier, inc=1, device_id={"layer": (layer + dl) % layers}, device_id_type=MESH
        )

    loads = [
        pltpu.make_async_copy(inv_hbm.at[0], inv.at[0], load_sem.at[0]),
        pltpu.make_async_copy(rhs_hbm.at[0], rhs.at[0], load_sem.at[1]),
        pltpu.make_async_copy(blocks_hbm.at[0], blocks0, load_sem.at[2]),
        pltpu.make_async_copy(inv_hbm.at[1], inv.at[1], load_sem.at[3]),
        pltpu.make_async_copy(rhs_hbm.at[1], rhs.at[1], load_sem.at[4]),
        pltpu.make_async_copy(blocks_hbm.at[1], blocks1, load_sem.at[5]),
        pltpu.make_async_copy(inv_anc_hbm, inv_anc, load_sem.at[6]),
        pltpu.make_async_copy(rhs_anc_hbm, rhs_anc, load_sem.at[7]),
    ]
    for load in loads:
        load.start()

    def listed(level, target):
        index, found = jnp.int32(0), jnp.int32(0)
        for s in range(slots):
            hit = (targets[level, s] == target).astype(jnp.int32)
            index = index + hit * s
            found = found + hit
        return (blocks0, blocks1)[level][index], found.astype(F32)

    def span(j):
        return pl.ds(pl.multiple_of(j * share, share), share)

    loads[0].wait()
    loads[1].wait()
    first = jnp.dot(inv[0], rhs[0], preferred_element_type=F32)
    x0[...] = first.T.astype(BF16)

    loads[2].wait()
    goal = (row + rows - 1) % rows
    active = goal < cols
    owner = (1 + col) % rows

    def p_copy(k):
        j = ordered(k)
        return pltpu.make_async_remote_copy(
            src_ref=part.at[j],
            dst_ref=part_in.at[col],
            send_sem=p_send.at[k],
            recv_sem=p_recv.at[col],
            device_id={"row": j, "col": goal},
            device_id_type=MESH,
        )

    pl.semaphore_wait(barrier, rows * cols - 1 + layers - 1)

    @pl.when(active)
    def _():
        block, found = listed(0, 1)
        for k in range(rows):
            j = ordered(k)
            value = dot_t(x0[span(j), :], block) * found
            part[j] = value.astype(BF16)
            if k == 0:

                @pl.when(goal != col)
                def _():
                    p_copy(0).start()

                @pl.when(goal == col)
                def _():
                    part_in[col] = part[row]

            else:
                p_copy(k).start()

    for j in range(rows):

        @pl.when(row == j)
        def _():
            low[0] = x0[j * share : (j + 1) * share, :].astype(F32).T.astype(BF16)

    low0 = pltpu.make_async_copy(low.at[0], low_out.at[0], out_sem.at[0])
    low0.start()

    for a in range(anc_row):
        block, found = listed(0, a + 2)
        base[:, a * width : (a + 1) * width] = dot_t(x0[...], block) * found

    loads[3].wait()
    loads[4].wait()
    for j in range(rows):

        @pl.when(row == j)
        def _():
            right[...] = rhs[1, :, j * share : (j + 1) * share].astype(F32).T

    for cc in range(cols):

        @pl.when(jnp.logical_or(col != cc, row != owner))
        def _():
            pltpu.make_async_remote_copy(
                src_ref=part.at[0],
                dst_ref=part_in.at[cc],
                send_sem=p_send.at[0],
                recv_sem=p_recv.at[cc],
                device_id={"row": row, "col": col},
                device_id_type=MESH,
            ).wait_recv()

    total = part_in[0].astype(F32)
    for cc in range(1, cols):
        total = total + part_in[cc].astype(F32)
    residual = (right[...] - total).astype(BF16)
    x1[row] = dot_t(residual, inv[1]).astype(BF16)

    def x_copy(k, slot):
        return pltpu.make_async_remote_copy(
            src_ref=x1.at[slot],
            dst_ref=x1.at[slot],
            send_sem=x_send.at[k],
            recv_sem=x_recv.at[slot],
            device_id={"row": ordered(k)},
            device_id_type=MESH,
        )

    for k in range(1, rows):
        x_copy(k, row).start()

    def y_copy(d, j):
        cc = (col + d) % cols
        return pltpu.make_async_remote_copy(
            src_ref=packed.at[cc, j],
            dst_ref=y_in.at[d - 1, j],
            send_sem=y_send.at[d - 1, j],
            recv_sem=y_recv.at[d - 1, j],
            device_id={"col": cc},
            device_id_type=MESH,
        )

    loads[5].wait()
    for k in range(rows):
        j = order[k]

        @pl.when(j != row)
        def _():
            x_copy(1, j).wait_recv()

        for a in range(anc_row):
            block, found = listed(1, a + 2)
            at = slice(a * width, (a + 1) * width)
            value = base[span(j), at] + dot_t(x1[j], block) * found
            value = value.astype(BF16)
            for cc in range(cols):
                packed[cc, j, :, at] = value[cc * narrow : (cc + 1) * narrow]
        for d in range(1, cols):
            y_copy(d, j).start()
        if k == 0:
            low[1] = x1[row].astype(F32).T.astype(BF16)
            low1 = pltpu.make_async_copy(low.at[1], low_out.at[1], out_sem.at[1])
            low1.start()

    def z_copy(j, slot, target):
        return pltpu.make_async_remote_copy(
            src_ref=z_out.at[j],
            dst_ref=z_in.at[slot],
            send_sem=z_send.at[j],
            recv_sem=z_recv.at[slot],
            device_id={"layer": target},
            device_id_type=MESH,
        )

    for k in range(rows):
        j = merge_order[k]
        for d in range(1, cols):
            y_copy(d, j).wait_recv()
        merged = packed[col, j].astype(F32)
        for d in range(1, cols):
            merged = merged + y_in[d - 1, j].astype(F32)

        @pl.when(jnp.logical_and(j == last, layer == 1))
        def _():
            z_copy(j, layers, layer).wait_recv()
            z_out[j] = (merged + z_in[layers].astype(F32)).astype(BF16)
            z_copy(j, layer, j).start()

        @pl.when(jnp.logical_and(j == 0, layer == last - 1))
        def _():
            z_copy(j, layers + 1, layer).wait_recv()
            z_out[j] = (merged + z_in[layers + 1].astype(F32)).astype(BF16)
            z_copy(j, layer, j).start()

        @pl.when(jnp.logical_and(j == last, layer == 0))
        def _():
            z_out[j] = merged.astype(BF16)
            z_copy(j, layers, 1).start()

        @pl.when(jnp.logical_and(j == 0, layer == last))
        def _():
            z_out[j] = merged.astype(BF16)
            z_copy(j, layers + 1, last - 1).start()

        direct = jnp.logical_and(j != layer, j != relayed)
        direct = jnp.logical_and(direct, jnp.abs(layer - j) != last)

        @pl.when(direct)
        def _():
            z_out[j] = merged.astype(BF16)
            z_copy(j, layer, j).start()

        @pl.when(j == layer)
        def _():
            z_in[layer] = merged.astype(BF16)

    loads[6].wait()
    loads[7].wait()
    for s in range(layers):

        @pl.when(jnp.abs(layer - s) == last)
        def _():
            z_in[s] = jnp.zeros_like(z_in[s])

        @pl.when(jnp.logical_and(layer != s, jnp.abs(layer - s) != last))
        def _():
            z_copy(s, s, layer).wait_recv()

    for a in range(anc_row):
        residual = rhs_anc[a].astype(F32)
        for s in range(layers):
            residual = residual - z_in[s, :, a * width : (a + 1) * width].astype(F32)
        anc_out[a] = dot_t(residual.astype(BF16), inv_anc[a])

    @pl.when(active)
    def _():
        for k in range(rows):
            if k == 0:

                @pl.when(goal != col)
                def _():
                    p_copy(0).wait_send()

            else:
                p_copy(k).wait_send()

    for k in range(1, rows):
        x_copy(k, row).wait_send()
    for k in range(rows):
        j = ordered(k)
        for d in range(1, cols):
            y_copy(d, j).wait_send()

        @pl.when(j != layer)
        def _():
            z_copy(j, layer, j).wait_send()

    low0.wait()
    low1.wait()


def on_device(sizes, rhs_low, inv_low, blocks, targets, rhs_anc, inv_anc):
    layers, rows, cols = sizes
    levels, slots = blocks.shape[3], blocks.shape[4]
    width, cases = rhs_low.shape[3], rhs_low.shape[4]
    anc_row, narrow = rhs_anc.shape[0], rhs_anc.shape[2]
    share = cases // rows
    assert levels == 2 and layers == rows and layers > 3 and cols <= rows and cols * narrow == share
    any_space = pl.BlockSpec(memory_space=pl.ANY)
    dma = pltpu.SemaphoreType.DMA
    low, anc = pl.pallas_call(
        functools.partial(kernel, sizes),
        out_shape=(
            jax.ShapeDtypeStruct((levels, width, share), BF16),
            jax.ShapeDtypeStruct((anc_row, narrow, width), F32),
        ),
        in_specs=[pl.BlockSpec(memory_space=pltpu.SMEM)] + [any_space] * 5,
        out_specs=(any_space, pl.BlockSpec(memory_space=pltpu.VMEM)),
        scratch_shapes=[
            pltpu.VMEM((levels, width, cases), BF16),
            pltpu.VMEM((levels, width, width), BF16),
            pltpu.VMEM((slots, width, width), BF16),
            pltpu.VMEM((slots, width, width), BF16),
            pltpu.VMEM((anc_row, narrow, width), BF16),
            pltpu.VMEM((anc_row, width, width), BF16),
            pltpu.VMEM((levels, width, share), BF16),
            pltpu.VMEM((cases, width), BF16),
            pltpu.VMEM((rows, share, width), BF16),
            pltpu.VMEM((rows, share, width), BF16),
            pltpu.VMEM((cols, share, width), BF16),
            pltpu.VMEM((share, width), F32),
            pltpu.VMEM((cases, anc_row * width), F32),
            pltpu.VMEM((cols, rows, narrow, anc_row * width), BF16),
            pltpu.VMEM((cols - 1, rows, narrow, anc_row * width), BF16),
            pltpu.VMEM((layers, narrow, anc_row * width), BF16),
            pltpu.VMEM((layers + 2, narrow, anc_row * width), BF16),
            dma((8,)),
            dma((2,)),
            dma((rows,)),
            dma((cols,)),
            dma((rows,)),
            dma((rows,)),
            dma((cols - 1, rows)),
            dma((cols - 1, rows)),
            dma((layers,)),
            dma((layers + 2,)),
        ],
        compiler_params=pltpu.CompilerParams(
            collective_id=0, has_side_effects=True, vmem_limit_bytes=56 * 1024 * 1024
        ),
    )(
        targets.reshape(levels, slots),
        rhs_low.reshape(levels, width, cases),
        inv_low.reshape(levels, width, width),
        blocks.reshape(levels, slots, width, width),
        rhs_anc.transpose(0, 2, 1),
        inv_anc,
    )
    return low[None, :, None], anc.transpose(0, 2, 1)


def solution(mesh):
    sizes = tuple(mesh.shape[a] for a in ("layer", "row", "col"))
    in_specs = (
        P("layer", None, "col", None, None),
        P("layer", None, "col", None, None),
        P("layer", "row", "col", None, None, None, None),
        P("layer", "row", "col", None, None),
        P("row", None, ("layer", "col")),
        P("row", None, None),
    )
    out_specs = (P("layer", None, "col", None, "row"), P("row", None, ("layer", "col")))
    return jax.shard_map(
        functools.partial(on_device, sizes),
        mesh=mesh,
        in_specs=in_specs,
        out_specs=out_specs,
        check_vma=False,
    )
```

```python
import functools

import jax
import jax.numpy as jnp
from jax import lax
from jax.experimental import pallas as pl
from jax.experimental.pallas import tpu as pltpu
from jax.sharding import PartitionSpec as P

MESH = pl.DeviceIdType.MESH
F32 = jnp.float32
BF16 = jnp.bfloat16


def dot_t(left, right):
    return lax.dot_general(left, right, (((1,), (1,)), ((), ())), preferred_element_type=F32)


def kernel(
    sizes,
    targets,
    rhs_hbm,
    inv_hbm,
    blocks_hbm,
    rhs_anc_hbm,
    inv_anc_hbm,
    low_out,
    anc_out,
    rhs,
    inv,
    blocks0,
    blocks1,
    rhs_anc,
    inv_anc,
    x0,
    x1,
    part,
    part_in,
    right,
    base,
    packed,
    y_in,
    z_out,
    z_in,
    load_sem,
    p_send,
    p_recv,
    x_send,
    x_recv,
    y_send,
    y_recv,
    z_send,
    z_recv,
):
    layers, rows, cols = sizes
    layer, row, col = (lax.axis_index(a) for a in ("layer", "row", "col"))
    slots = blocks0.shape[0]
    anc_row, narrow, width = rhs_anc.shape
    share = x1.shape[1]

    def ordered(k):
        return (row // 2 * 2 + k // 2 * 2) % rows + (row + k) % 2

    def flag(condition):
        return condition.astype(jnp.int32)

    last = layers - 1
    relayed = flag(layer == 1) * last - flag(layer != 1)
    relayed = relayed + flag(layer == last - 1) * (0 - relayed)
    opening = row + flag(row == layer) * (ordered(1) - row)
    keys = []
    for j in range(rows):
        place = 0
        for k in range(rows):
            place = place + k * flag(ordered(k) == j)
        key = place - 16 * jnp.abs(layer - j)
        key = key + 500 * flag(relayed == j) + 5000 * flag(layer == j) - 2000 * flag(opening == j)
        keys.append(key)
    order = [0] * rows
    for j in range(rows):
        rank = 0
        for other in range(rows):
            if other != j:
                rank = rank + flag(keys[other] < keys[j])
        order = [order[k] + j * flag(rank == k) for k in range(rows)]
    swap = flag(relayed == opening) * (order[1] - order[0])
    merge_order = [order[0] + swap, order[1] - swap] + order[2:]

    barrier = pltpu.get_barrier_semaphore()
    for dr in range(rows):
        for dc in range(cols):
            if dr or dc:
                pl.semaphore_signal(
                    barrier,
                    inc=1,
                    device_id={"row": (row + dr) % rows, "col": (col + dc) % cols},
                    device_id_type=MESH,
                )
    for dl in range(1, layers):
        pl.semaphore_signal(
            barrier, inc=1, device_id={"layer": (layer + dl) % layers}, device_id_type=MESH
        )

    loads = [
        pltpu.make_async_copy(inv_hbm.at[0], inv.at[0], load_sem.at[0]),
        pltpu.make_async_copy(rhs_hbm.at[0], rhs.at[0], load_sem.at[1]),
        pltpu.make_async_copy(blocks_hbm.at[0], blocks0, load_sem.at[2]),
        pltpu.make_async_copy(inv_hbm.at[1], inv.at[1], load_sem.at[3]),
        pltpu.make_async_copy(rhs_hbm.at[1], rhs.at[1], load_sem.at[4]),
        pltpu.make_async_copy(blocks_hbm.at[1], blocks1, load_sem.at[5]),
        pltpu.make_async_copy(inv_anc_hbm, inv_anc, load_sem.at[6]),
        pltpu.make_async_copy(rhs_anc_hbm, rhs_anc, load_sem.at[7]),
    ]
    for load in loads:
        load.start()

    def listed(level, target):
        index, found = jnp.int32(0), jnp.int32(0)
        for s in range(slots):
            hit = (targets[level, s] == target).astype(jnp.int32)
            index = index + hit * s
            found = found + hit
        return (blocks0, blocks1)[level][index], found.astype(F32)

    def span(j):
        return pl.ds(pl.multiple_of(j * share, share), share)

    loads[0].wait()
    loads[1].wait()
    first = jnp.dot(inv[0], rhs[0], preferred_element_type=F32)
    x0[...] = first.T.astype(BF16)

    loads[2].wait()
    goal = (row + rows - 1) % rows
    active = goal < cols
    owner = (1 + col) % rows

    def p_copy(k):
        j = ordered(k)
        return pltpu.make_async_remote_copy(
            src_ref=part.at[j],
            dst_ref=part_in.at[col],
            send_sem=p_send.at[k],
            recv_sem=p_recv.at[col],
            device_id={"row": j, "col": goal},
            device_id_type=MESH,
        )

    pl.semaphore_wait(barrier, rows * cols - 1 + layers - 1)

    @pl.when(active)
    def _():
        block, found = listed(0, 1)
        for k in range(rows):
            j = ordered(k)
            value = dot_t(x0[span(j), :], block) * found
            part[j] = value.astype(BF16)
            if k == 0:

                @pl.when(goal != col)
                def _():
                    p_copy(0).start()

                @pl.when(goal == col)
                def _():
                    part_in[col] = part[row]

            else:
                p_copy(k).start()

    for j in range(rows):

        @pl.when(row == j)
        def _():
            low_out[0] = x0[j * share : (j + 1) * share, :].astype(F32).T.astype(BF16)

    for a in range(anc_row):
        block, found = listed(0, a + 2)
        base[:, a * width : (a + 1) * width] = dot_t(x0[...], block) * found

    loads[3].wait()
    loads[4].wait()
    for j in range(rows):

        @pl.when(row == j)
        def _():
            right[...] = rhs[1, :, j * share : (j + 1) * share].astype(F32).T

    for cc in range(cols):

        @pl.when(jnp.logical_or(col != cc, row != owner))
        def _():
            pltpu.make_async_remote_copy(
                src_ref=part.at[0],
                dst_ref=part_in.at[cc],
                send_sem=p_send.at[0],
                recv_sem=p_recv.at[cc],
                device_id={"row": row, "col": col},
                device_id_type=MESH,
            ).wait_recv()

    total = part_in[0].astype(F32)
    for cc in range(1, cols):
        total = total + part_in[cc].astype(F32)
    residual = (right[...] - total).astype(BF16)
    x1[row] = dot_t(residual, inv[1]).astype(BF16)

    def x_copy(k, slot):
        return pltpu.make_async_remote_copy(
            src_ref=x1.at[slot],
            dst_ref=x1.at[slot],
            send_sem=x_send.at[k],
            recv_sem=x_recv.at[slot],
            device_id={"row": ordered(k)},
            device_id_type=MESH,
        )

    for k in range(1, rows):
        x_copy(k, row).start()

    def y_copy(d, j):
        cc = (col + d) % cols
        return pltpu.make_async_remote_copy(
            src_ref=packed.at[cc, j],
            dst_ref=y_in.at[d - 1, j],
            send_sem=y_send.at[d - 1, j],
            recv_sem=y_recv.at[d - 1, j],
            device_id={"col": cc},
            device_id_type=MESH,
        )

    loads[5].wait()
    for k in range(rows):
        j = order[k]

        @pl.when(j != row)
        def _():
            x_copy(1, j).wait_recv()

        for a in range(anc_row):
            block, found = listed(1, a + 2)
            at = slice(a * width, (a + 1) * width)
            value = base[span(j), at] + dot_t(x1[j], block) * found
            value = value.astype(BF16)
            for cc in range(cols):
                packed[cc, j, :, at] = value[cc * narrow : (cc + 1) * narrow]
        for d in range(1, cols):
            y_copy(d, j).start()
        if k == 0:
            low_out[1] = x1[row].astype(F32).T.astype(BF16)

    def z_copy(j, slot, target):
        return pltpu.make_async_remote_copy(
            src_ref=z_out.at[j],
            dst_ref=z_in.at[slot],
            send_sem=z_send.at[j],
            recv_sem=z_recv.at[slot],
            device_id={"layer": target},
            device_id_type=MESH,
        )

    for k in range(rows):
        j = merge_order[k]
        for d in range(1, cols):
            y_copy(d, j).wait_recv()
        merged = packed[col, j].astype(F32)
        for d in range(1, cols):
            merged = merged + y_in[d - 1, j].astype(F32)

        @pl.when(jnp.logical_and(j == last, layer == 1))
        def _():
            z_copy(j, layers, layer).wait_recv()
            z_out[j] = (merged + z_in[layers].astype(F32)).astype(BF16)
            z_copy(j, layer, j).start()

        @pl.when(jnp.logical_and(j == 0, layer == last - 1))
        def _():
            z_copy(j, layers + 1, layer).wait_recv()
            z_out[j] = (merged + z_in[layers + 1].astype(F32)).astype(BF16)
            z_copy(j, layer, j).start()

        @pl.when(jnp.logical_and(j == last, layer == 0))
        def _():
            z_out[j] = merged.astype(BF16)
            z_copy(j, layers, 1).start()

        @pl.when(jnp.logical_and(j == 0, layer == last))
        def _():
            z_out[j] = merged.astype(BF16)
            z_copy(j, layers + 1, last - 1).start()

        direct = jnp.logical_and(j != layer, j != relayed)
        direct = jnp.logical_and(direct, jnp.abs(layer - j) != last)

        @pl.when(direct)
        def _():
            z_out[j] = merged.astype(BF16)
            z_copy(j, layer, j).start()

        @pl.when(j == layer)
        def _():
            z_in[layer] = merged.astype(BF16)

    loads[6].wait()
    loads[7].wait()
    for s in range(layers):

        @pl.when(jnp.abs(layer - s) == last)
        def _():
            z_in[s] = jnp.zeros_like(z_in[s])

        @pl.when(jnp.logical_and(layer != s, jnp.abs(layer - s) != last))
        def _():
            z_copy(s, s, layer).wait_recv()

    for a in range(anc_row):
        residual = rhs_anc[a].astype(F32)
        for s in range(layers):
            residual = residual - z_in[s, :, a * width : (a + 1) * width].astype(F32)
        anc_out[a] = dot_t(residual.astype(BF16), inv_anc[a])


    @pl.when(active)
    def _():
        for k in range(rows):
            if k == 0:

                @pl.when(goal != col)
                def _():
                    p_copy(0).wait_send()

            else:
                p_copy(k).wait_send()

    for k in range(1, rows):
        x_copy(k, row).wait_send()
    for k in range(rows):
        j = ordered(k)
        for d in range(1, cols):
            y_copy(d, j).wait_send()

        @pl.when(j != layer)
        def _():
            z_copy(j, layer, j).wait_send()


def hand_over(low, anc, low_out, anc_out, sem):
    first = pltpu.make_async_copy(anc, anc_out, sem.at[0])
    second = pltpu.make_async_copy(low, low_out, sem.at[1])
    first.start()
    second.start()
    first.wait()
    second.wait()


def on_device(sizes, rhs_low, inv_low, blocks, targets, rhs_anc, inv_anc):
    layers, rows, cols = sizes
    levels, slots = blocks.shape[3], blocks.shape[4]
    width, cases = rhs_low.shape[3], rhs_low.shape[4]
    anc_row, narrow = rhs_anc.shape[0], rhs_anc.shape[2]
    share = cases // rows
    assert levels == 2 and layers == rows and layers > 3 and cols <= rows and cols * narrow == share
    any_space = pl.BlockSpec(memory_space=pltpu.HBM)
    dma = pltpu.SemaphoreType.DMA
    low, anc = pl.pallas_call(
        functools.partial(kernel, sizes),
        out_shape=(
            pltpu.VMEM((levels, width, share), BF16),
            pltpu.VMEM((anc_row, narrow, width), F32),
        ),
        in_specs=[pl.BlockSpec(memory_space=pltpu.SMEM)] + [any_space] * 5,
        out_specs=(pl.BlockSpec(memory_space=pltpu.VMEM), pl.BlockSpec(memory_space=pltpu.VMEM)),
        scratch_shapes=[
            pltpu.VMEM((levels, width, cases), BF16),
            pltpu.VMEM((levels, width, width), BF16),
            pltpu.VMEM((slots, width, width), BF16),
            pltpu.VMEM((slots, width, width), BF16),
            pltpu.VMEM((anc_row, narrow, width), BF16),
            pltpu.VMEM((anc_row, width, width), BF16),
            pltpu.VMEM((cases, width), BF16),
            pltpu.VMEM((rows, share, width), BF16),
            pltpu.VMEM((rows, share, width), BF16),
            pltpu.VMEM((cols, share, width), BF16),
            pltpu.VMEM((share, width), F32),
            pltpu.VMEM((cases, anc_row * width), F32),
            pltpu.VMEM((cols, rows, narrow, anc_row * width), BF16),
            pltpu.VMEM((cols - 1, rows, narrow, anc_row * width), BF16),
            pltpu.VMEM((layers, narrow, anc_row * width), BF16),
            pltpu.VMEM((layers + 2, narrow, anc_row * width), BF16),
            dma((8,)),
            dma((rows,)),
            dma((cols,)),
            dma((rows,)),
            dma((rows,)),
            dma((cols - 1, rows)),
            dma((cols - 1, rows)),
            dma((layers,)),
            dma((layers + 2,)),
        ],
        compiler_params=pltpu.CompilerParams(
            collective_id=0, has_side_effects=True, vmem_limit_bytes=56 * 1024 * 1024
        ),
    )(
        targets.reshape(levels, slots),
        rhs_low.reshape(levels, width, cases),
        inv_low.reshape(levels, width, width),
        blocks.reshape(levels, slots, width, width),
        rhs_anc.transpose(0, 2, 1),
        inv_anc,
    )
    low, anc = pl.pallas_call(
        hand_over,
        out_shape=(
            jax.ShapeDtypeStruct(low.shape, low.dtype),
            jax.ShapeDtypeStruct(anc.shape, anc.dtype),
        ),
        in_specs=[pl.BlockSpec(memory_space=pltpu.VMEM)] * 2,
        out_specs=(any_space, any_space),
        scratch_shapes=[dma((2,))],
        compiler_params=pltpu.CompilerParams(vmem_limit_bytes=4 * 1024 * 1024),
    )(low, anc)
    return low[None, :, None], anc.transpose(0, 2, 1)


def solution(mesh):
    sizes = tuple(mesh.shape[a] for a in ("layer", "row", "col"))
    in_specs = (
        P("layer", None, "col", None, None),
        P("layer", None, "col", None, None),
        P("layer", "row", "col", None, None, None, None),
        P("layer", "row", "col", None, None),
        P("row", None, ("layer", "col")),
        P("row", None, None),
    )
    out_specs = (P("layer", None, "col", None, "row"), P("row", None, ("layer", "col")))
    return jax.shard_map(
        functools.partial(on_device, sizes),
        mesh=mesh,
        in_specs=in_specs,
        out_specs=out_specs,
        check_vma=False,
    )
```

```python
import functools

import jax
import jax.numpy as jnp
from jax import lax
from jax.experimental import pallas as pl
from jax.experimental.pallas import tpu as pltpu
from jax.sharding import PartitionSpec as P

MESH = pl.DeviceIdType.MESH
F32 = jnp.float32
BF16 = jnp.bfloat16


def dot_t(left, right):
    return lax.dot_general(left, right, (((1,), (1,)), ((), ())), preferred_element_type=F32)


def kernel(
    sizes,
    targets_hbm,
    rhs_hbm,
    inv_hbm,
    blocks_hbm,
    rhs_anc_hbm,
    inv_anc_hbm,
    low_out,
    anc_out,
    rhs,
    inv,
    blocks0,
    blocks1,
    rhs_anc,
    inv_anc,
    x0,
    x1,
    part,
    part_in,
    right,
    base,
    packed,
    y_in,
    z_out,
    z_in,
    targets,
    load_sem,
    p_send,
    p_recv,
    x_send,
    x_recv,
    y_send,
    y_recv,
    z_send,
    z_recv,
):
    layers, rows, cols = sizes
    layer, row, col = (lax.axis_index(a) for a in ("layer", "row", "col"))
    slots = blocks0.shape[0]
    anc_row, narrow, width = rhs_anc.shape
    share = x1.shape[1]
    halves = packed.shape[2]
    per_half = anc_row // halves

    def ordered(k):
        return (row // 2 * 2 + k // 2 * 2) % rows + (row + k) % 2

    def flag(condition):
        return condition.astype(jnp.int32)

    last = layers - 1
    relayed = flag(layer == 1) * last - flag(layer != 1)
    relayed = relayed + flag(layer == last - 1) * (0 - relayed)
    opening = row + flag(row == layer) * (ordered(1) - row)
    keys = []
    for j in range(rows):
        place = 0
        for k in range(rows):
            place = place + k * flag(ordered(k) == j)
        key = place - 16 * jnp.abs(layer - j)
        key = key + 500 * flag(relayed == j) + 5000 * flag(layer == j) - 2000 * flag(opening == j)
        keys.append(key)
    order = [0] * rows
    for j in range(rows):
        rank = 0
        for other in range(rows):
            if other != j:
                rank = rank + flag(keys[other] < keys[j])
        order = [order[k] + j * flag(rank == k) for k in range(rows)]
    swap = flag(relayed == opening) * (order[1] - order[0])
    merge_order = [order[0] + swap, order[1] - swap] + order[2:]

    barrier = pltpu.get_barrier_semaphore()
    for dr in range(rows):
        for dc in range(cols):
            if dr or dc:
                pl.semaphore_signal(
                    barrier,
                    inc=1,
                    device_id={"row": (row + dr) % rows, "col": (col + dc) % cols},
                    device_id_type=MESH,
                )
    for dl in range(1, layers):
        pl.semaphore_signal(
            barrier, inc=1, device_id={"layer": (layer + dl) % layers}, device_id_type=MESH
        )

    loads = [
        pltpu.make_async_copy(inv_hbm.at[0], inv.at[0], load_sem.at[0]),
        pltpu.make_async_copy(rhs_hbm.at[0], rhs.at[0], load_sem.at[1]),
        pltpu.make_async_copy(blocks_hbm.at[0], blocks0, load_sem.at[2]),
        pltpu.make_async_copy(inv_hbm.at[1], inv.at[1], load_sem.at[3]),
        pltpu.make_async_copy(rhs_hbm.at[1], rhs.at[1], load_sem.at[4]),
        pltpu.make_async_copy(blocks_hbm.at[1], blocks1, load_sem.at[5]),
        pltpu.make_async_copy(inv_anc_hbm, inv_anc, load_sem.at[6]),
        pltpu.make_async_copy(rhs_anc_hbm, rhs_anc, load_sem.at[7]),
        pltpu.make_async_copy(targets_hbm, targets, load_sem.at[8]),
    ]
    for load in loads:
        load.start()

    def listed(level, target):
        index, found = jnp.int32(0), jnp.int32(0)
        for s in range(slots):
            hit = (targets[level, s] == target).astype(jnp.int32)
            index = index + hit * s
            found = found + hit
        return (blocks0, blocks1)[level][index], found.astype(F32)

    def span(j):
        return pl.ds(pl.multiple_of(j * share, share), share)

    loads[0].wait()
    loads[1].wait()
    first = jnp.dot(inv[0], rhs[0], preferred_element_type=F32)
    x0[...] = first.T.astype(BF16)

    loads[8].wait()
    loads[2].wait()
    goal = (row + rows - 1) % rows
    active = goal < cols
    owner = (1 + col) % rows

    def p_copy(k):
        j = ordered(k)
        return pltpu.make_async_remote_copy(
            src_ref=part.at[j],
            dst_ref=part_in.at[col],
            send_sem=p_send.at[k],
            recv_sem=p_recv.at[col],
            device_id={"row": j, "col": goal},
            device_id_type=MESH,
        )

    pl.semaphore_wait(barrier, rows * cols - 1 + layers - 1)

    @pl.when(active)
    def _():
        block, found = listed(0, 1)
        for k in range(rows):
            j = ordered(k)
            value = dot_t(x0[span(j), :], block) * found
            part[j] = value.astype(BF16)
            if k == 0:

                @pl.when(goal != col)
                def _():
                    p_copy(0).start()

                @pl.when(goal == col)
                def _():
                    part_in[col] = part[row]

            else:
                p_copy(k).start()

    for j in range(rows):

        @pl.when(row == j)
        def _():
            low_out[0] = x0[j * share : (j + 1) * share, :].astype(F32).T.astype(BF16)

    for a in range(anc_row):
        block, found = listed(0, a + 2)
        base[:, a * width : (a + 1) * width] = dot_t(x0[...], block) * found

    loads[3].wait()
    loads[4].wait()
    for j in range(rows):

        @pl.when(row == j)
        def _():
            right[...] = rhs[1, :, j * share : (j + 1) * share].astype(F32).T

    for cc in range(cols):

        @pl.when(jnp.logical_or(col != cc, row != owner))
        def _():
            pltpu.make_async_remote_copy(
                src_ref=part.at[0],
                dst_ref=part_in.at[cc],
                send_sem=p_send.at[0],
                recv_sem=p_recv.at[cc],
                device_id={"row": row, "col": col},
                device_id_type=MESH,
            ).wait_recv()

    total = part_in[0].astype(F32)
    for cc in range(1, cols):
        total = total + part_in[cc].astype(F32)
    residual = (right[...] - total).astype(BF16)
    x1[row] = dot_t(residual, inv[1]).astype(BF16)

    def x_copy(k, slot):
        return pltpu.make_async_remote_copy(
            src_ref=x1.at[slot],
            dst_ref=x1.at[slot],
            send_sem=x_send.at[k],
            recv_sem=x_recv.at[slot],
            device_id={"row": ordered(k)},
            device_id_type=MESH,
        )

    for k in range(1, rows):
        x_copy(k, row).start()

    def y_copy(d, j, h):
        cc = (col + d) % cols
        return pltpu.make_async_remote_copy(
            src_ref=packed.at[cc, j, h],
            dst_ref=y_in.at[d - 1, j, h],
            send_sem=y_send.at[d - 1, j, h],
            recv_sem=y_recv.at[d - 1, j, h],
            device_id={"col": cc},
            device_id_type=MESH,
        )

    loads[5].wait()
    for k in range(rows):
        j = order[k]

        @pl.when(j != row)
        def _():
            x_copy(1, j).wait_recv()

        for a in range(anc_row):
            block, found = listed(1, a + 2)
            at = slice(a * width, (a + 1) * width)
            value = base[span(j), at] + dot_t(x1[j], block) * found
            value = value.astype(BF16)
            for cc in range(cols):
                within = a % per_half * width
                packed[cc, j, a // per_half, :, within : within + width] = value[
                    cc * narrow : (cc + 1) * narrow
                ]
            if a % per_half == per_half - 1:
                for d in range(1, cols):
                    y_copy(d, j, a // per_half).start()
        if k == 0:
            low_out[1] = x1[row].astype(F32).T.astype(BF16)

    def z_copy(j, slot, target, h):
        return pltpu.make_async_remote_copy(
            src_ref=z_out.at[j, h],
            dst_ref=z_in.at[slot, h],
            send_sem=z_send.at[j, h],
            recv_sem=z_recv.at[slot, h],
            device_id={"layer": target},
            device_id_type=MESH,
        )

    def merge(j, h):
        for d in range(1, cols):
            y_copy(d, j, h).wait_recv()
        merged = packed[col, j, h].astype(F32)
        for d in range(1, cols):
            merged = merged + y_in[d - 1, j, h].astype(F32)

        @pl.when(jnp.logical_and(j == last, layer == 1))
        def _():
            z_copy(j, layers, layer, h).wait_recv()
            z_out[j, h] = (merged + z_in[layers, h].astype(F32)).astype(BF16)
            z_copy(j, layer, j, h).start()

        @pl.when(jnp.logical_and(j == 0, layer == last - 1))
        def _():
            z_copy(j, layers + 1, layer, h).wait_recv()
            z_out[j, h] = (merged + z_in[layers + 1, h].astype(F32)).astype(BF16)
            z_copy(j, layer, j, h).start()

        @pl.when(jnp.logical_and(j == last, layer == 0))
        def _():
            z_out[j, h] = merged.astype(BF16)
            z_copy(j, layers, 1, h).start()

        @pl.when(jnp.logical_and(j == 0, layer == last))
        def _():
            z_out[j, h] = merged.astype(BF16)
            z_copy(j, layers + 1, last - 1, h).start()

        direct = jnp.logical_and(j != layer, j != relayed)
        direct = jnp.logical_and(direct, jnp.abs(layer - j) != last)

        @pl.when(direct)
        def _():
            z_out[j, h] = merged.astype(BF16)
            z_copy(j, layer, j, h).start()

        @pl.when(j == layer)
        def _():
            z_in[layer, h] = merged.astype(BF16)

    for j in merge_order:
        for h in range(halves):
            merge(j, h)

    loads[6].wait()
    loads[7].wait()
    for s in range(layers):

        @pl.when(jnp.abs(layer - s) == last)
        def _():
            z_in[s] = jnp.zeros_like(z_in[s])

        @pl.when(jnp.logical_and(layer != s, jnp.abs(layer - s) != last))
        def _():
            for h in range(halves):
                z_copy(s, s, layer, h).wait_recv()

    for a in range(anc_row):
        residual = rhs_anc[a].astype(F32)
        for s in range(layers):
            within = a % per_half * width
            piece = z_in[s, a // per_half, :, within : within + width]
            residual = residual - piece.astype(F32)
        anc_out[a] = dot_t(residual.astype(BF16), inv_anc[a])


    @pl.when(active)
    def _():
        for k in range(rows):
            if k == 0:

                @pl.when(goal != col)
                def _():
                    p_copy(0).wait_send()

            else:
                p_copy(k).wait_send()

    for k in range(1, rows):
        x_copy(k, row).wait_send()
    for k in range(rows):
        j = ordered(k)
        for d in range(1, cols):
            for h in range(halves):
                y_copy(d, j, h).wait_send()

        @pl.when(j != layer)
        def _():
            for h in range(halves):
                z_copy(j, layer, j, h).wait_send()


def hand_over(low, anc, low_out, anc_out, sem):
    first = pltpu.make_async_copy(anc, anc_out, sem.at[0])
    second = pltpu.make_async_copy(low, low_out, sem.at[1])
    first.start()
    second.start()
    first.wait()
    second.wait()


def on_device(sizes, rhs_low, inv_low, blocks, targets, rhs_anc, inv_anc):
    layers, rows, cols = sizes
    levels, slots = blocks.shape[3], blocks.shape[4]
    width, cases = rhs_low.shape[3], rhs_low.shape[4]
    anc_row, narrow = rhs_anc.shape[0], rhs_anc.shape[2]
    share = cases // rows
    halves = 2 if anc_row % 2 == 0 else 1
    assert levels == 2 and layers == rows and layers > 3 and cols <= rows and cols * narrow == share
    any_space = pl.BlockSpec(memory_space=pltpu.HBM)
    dma = pltpu.SemaphoreType.DMA
    low, anc = pl.pallas_call(
        functools.partial(kernel, sizes),
        out_shape=(
            pltpu.VMEM((levels, width, share), BF16),
            pltpu.VMEM((anc_row, narrow, width), F32),
        ),
        in_specs=[any_space] * 6,
        out_specs=(pl.BlockSpec(memory_space=pltpu.VMEM), pl.BlockSpec(memory_space=pltpu.VMEM)),
        scratch_shapes=[
            pltpu.VMEM((levels, width, cases), BF16),
            pltpu.VMEM((levels, width, width), BF16),
            pltpu.VMEM((slots, width, width), BF16),
            pltpu.VMEM((slots, width, width), BF16),
            pltpu.VMEM((anc_row, narrow, width), BF16),
            pltpu.VMEM((anc_row, width, width), BF16),
            pltpu.VMEM((cases, width), BF16),
            pltpu.VMEM((rows, share, width), BF16),
            pltpu.VMEM((rows, share, width), BF16),
            pltpu.VMEM((cols, share, width), BF16),
            pltpu.VMEM((share, width), F32),
            pltpu.VMEM((cases, anc_row * width), F32),
            pltpu.VMEM((cols, rows, halves, narrow, anc_row * width // halves), BF16),
            pltpu.VMEM((cols - 1, rows, halves, narrow, anc_row * width // halves), BF16),
            pltpu.VMEM((layers, halves, narrow, anc_row * width // halves), BF16),
            pltpu.VMEM((layers + 2, halves, narrow, anc_row * width // halves), BF16),
            pltpu.SMEM((levels, slots), jnp.int32),
            dma((9,)),
            dma((rows,)),
            dma((cols,)),
            dma((rows,)),
            dma((rows,)),
            dma((cols - 1, rows, halves)),
            dma((cols - 1, rows, halves)),
            dma((layers, halves)),
            dma((layers + 2, halves)),
        ],
        compiler_params=pltpu.CompilerParams(
            collective_id=0, has_side_effects=True, vmem_limit_bytes=56 * 1024 * 1024
        ),
    )(
        targets.reshape(levels, slots),
        rhs_low.reshape(levels, width, cases),
        inv_low.reshape(levels, width, width),
        blocks.reshape(levels, slots, width, width),
        rhs_anc.transpose(0, 2, 1),
        inv_anc,
    )
    low, anc = pl.pallas_call(
        hand_over,
        out_shape=(
            jax.ShapeDtypeStruct(low.shape, low.dtype),
            jax.ShapeDtypeStruct(anc.shape, anc.dtype),
        ),
        in_specs=[pl.BlockSpec(memory_space=pltpu.VMEM)] * 2,
        out_specs=(any_space, any_space),
        scratch_shapes=[dma((2,))],
        compiler_params=pltpu.CompilerParams(vmem_limit_bytes=4 * 1024 * 1024),
    )(low, anc)
    return low[None, :, None], anc.transpose(0, 2, 1)


def solution(mesh):
    sizes = tuple(mesh.shape[a] for a in ("layer", "row", "col"))
    in_specs = (
        P("layer", None, "col", None, None),
        P("layer", None, "col", None, None),
        P("layer", "row", "col", None, None, None, None),
        P("layer", "row", "col", None, None),
        P("row", None, ("layer", "col")),
        P("row", None, None),
    )
    out_specs = (P("layer", None, "col", None, "row"), P("row", None, ("layer", "col")))
    return jax.shard_map(
        functools.partial(on_device, sizes),
        mesh=mesh,
        in_specs=in_specs,
        out_specs=out_specs,
        check_vma=False,
    )
```

```python
import functools

import jax
import jax.numpy as jnp
from jax import lax
from jax.experimental import pallas as pl
from jax.experimental.pallas import tpu as pltpu
from jax.sharding import PartitionSpec as P

MESH = pl.DeviceIdType.MESH
F32 = jnp.float32
BF16 = jnp.bfloat16


def dot_t(left, right):
    return lax.dot_general(left, right, (((1,), (1,)), ((), ())), preferred_element_type=F32)


def kernel(
    sizes,
    targets_hbm,
    rhs_hbm,
    inv_hbm,
    blocks_hbm,
    rhs_anc_hbm,
    inv_anc_hbm,
    low_out,
    anc_out,
    rhs,
    inv,
    blocks0,
    blocks1,
    rhs_anc,
    inv_anc,
    x0,
    x1,
    part,
    part_in,
    right,
    base,
    packed,
    y_in,
    z_out,
    z_in,
    targets,
    load_sem,
    p_send,
    p_recv,
    x_send,
    x_recv,
    y_send,
    y_recv,
    z_send,
    z_recv,
):
    layers, rows, cols = sizes
    layer, row, col = (lax.axis_index(a) for a in ("layer", "row", "col"))
    slots = blocks0.shape[0]
    anc_row, narrow, width = rhs_anc.shape
    share = x1.shape[1]
    halves = packed.shape[2]
    per_half = anc_row // halves

    def ordered(k):
        return (row // 2 * 2 + k // 2 * 2) % rows + (row + k) % 2

    def flag(condition):
        return condition.astype(jnp.int32)

    last = layers - 1
    relayed = flag(layer == 1) * last - flag(layer != 1)
    relayed = relayed + flag(layer == last - 1) * (0 - relayed)
    opening = row + flag(row == layer) * (ordered(1) - row)
    keys = []
    for j in range(rows):
        place = 0
        for k in range(rows):
            place = place + k * flag(ordered(k) == j)
        key = place - 16 * jnp.abs(layer - j)
        key = key + 500 * flag(relayed == j) + 5000 * flag(layer == j) - 2000 * flag(opening == j)
        keys.append(key)
    order = [0] * rows
    for j in range(rows):
        rank = 0
        for other in range(rows):
            if other != j:
                rank = rank + flag(keys[other] < keys[j])
        order = [order[k] + j * flag(rank == k) for k in range(rows)]
    swap = flag(relayed == opening) * (order[1] - order[0])
    merge_order = [order[0] + swap, order[1] - swap] + order[2:]

    barrier = pltpu.get_barrier_semaphore()
    for dr in range(rows):
        for dc in range(cols):
            if dr or dc:
                pl.semaphore_signal(
                    barrier,
                    inc=1,
                    device_id={"row": (row + dr) % rows, "col": (col + dc) % cols},
                    device_id_type=MESH,
                )
    for dl in range(1, layers):
        pl.semaphore_signal(
            barrier, inc=1, device_id={"layer": (layer + dl) % layers}, device_id_type=MESH
        )

    loads = [
        pltpu.make_async_copy(inv_hbm.at[0], inv.at[0], load_sem.at[0]),
        pltpu.make_async_copy(rhs_hbm.at[0], rhs.at[0], load_sem.at[1]),
        pltpu.make_async_copy(blocks_hbm.at[0], blocks0, load_sem.at[2]),
        pltpu.make_async_copy(inv_hbm.at[1], inv.at[1], load_sem.at[3]),
        pltpu.make_async_copy(rhs_hbm.at[1], rhs.at[1], load_sem.at[4]),
        pltpu.make_async_copy(blocks_hbm.at[1], blocks1, load_sem.at[5]),
        pltpu.make_async_copy(inv_anc_hbm, inv_anc, load_sem.at[6]),
        pltpu.make_async_copy(rhs_anc_hbm, rhs_anc, load_sem.at[7]),
        pltpu.make_async_copy(targets_hbm, targets, load_sem.at[8]),
    ]
    for load in loads:
        load.start()

    def listed(level, target):
        index, found = jnp.int32(0), jnp.int32(0)
        for s in range(slots):
            hit = (targets[level, s] == target).astype(jnp.int32)
            index = index + hit * s
            found = found + hit
        return (blocks0, blocks1)[level][index], found.astype(F32)

    def span(j):
        return pl.ds(pl.multiple_of(j * share, share), share)

    loads[0].wait()
    loads[1].wait()
    first = jnp.dot(inv[0], rhs[0], preferred_element_type=F32)
    x0[...] = first.T.astype(BF16)

    loads[8].wait()
    loads[2].wait()
    goal = (row + rows - 1) % rows
    active = goal < cols
    owner = (1 + col) % rows

    def p_copy(k):
        j = ordered(k)
        return pltpu.make_async_remote_copy(
            src_ref=part.at[j],
            dst_ref=part_in.at[col],
            send_sem=p_send.at[k],
            recv_sem=p_recv.at[col],
            device_id={"row": j, "col": goal},
            device_id_type=MESH,
        )

    pl.semaphore_wait(barrier, rows * cols - 1 + layers - 1)

    @pl.when(active)
    def _():
        block, found = listed(0, 1)
        for k in range(rows):
            j = ordered(k)
            value = dot_t(x0[span(j), :], block) * found
            part[j] = value.astype(BF16)
            if k == 0:

                @pl.when(goal != col)
                def _():
                    p_copy(0).start()

                @pl.when(goal == col)
                def _():
                    part_in[col] = part[row]

            else:
                p_copy(k).start()

    for j in range(rows):

        @pl.when(row == j)
        def _():
            low_out[0] = x0[j * share : (j + 1) * share, :].astype(F32).T.astype(BF16)

    for a in range(anc_row):
        block, found = listed(0, a + 2)
        base[:, a * width : (a + 1) * width] = dot_t(x0[...], block) * found

    loads[3].wait()
    loads[4].wait()
    for j in range(rows):

        @pl.when(row == j)
        def _():
            right[...] = rhs[1, :, j * share : (j + 1) * share].astype(F32).T

    for cc in range(cols):

        @pl.when(jnp.logical_or(col != cc, row != owner))
        def _():
            pltpu.make_async_remote_copy(
                src_ref=part.at[0],
                dst_ref=part_in.at[cc],
                send_sem=p_send.at[0],
                recv_sem=p_recv.at[cc],
                device_id={"row": row, "col": col},
                device_id_type=MESH,
            ).wait_recv()

    total = part_in[0].astype(F32)
    for cc in range(1, cols):
        total = total + part_in[cc].astype(F32)
    residual = (right[...] - total).astype(BF16)
    x1[row] = dot_t(residual, inv[1]).astype(BF16)

    def x_copy(k, slot):
        return pltpu.make_async_remote_copy(
            src_ref=x1.at[slot],
            dst_ref=x1.at[slot],
            send_sem=x_send.at[k],
            recv_sem=x_recv.at[slot],
            device_id={"row": ordered(k)},
            device_id_type=MESH,
        )

    for k in range(1, rows):
        x_copy(k, row).start()

    def y_copy(d, j, h):
        cc = (col + d) % cols
        return pltpu.make_async_remote_copy(
            src_ref=packed.at[cc, j, h],
            dst_ref=y_in.at[d - 1, j, h],
            send_sem=y_send.at[d - 1, j, h],
            recv_sem=y_recv.at[d - 1, j, h],
            device_id={"col": cc},
            device_id_type=MESH,
        )

    loads[5].wait()
    for k in range(rows):
        j = order[k]

        @pl.when(j != row)
        def _():
            x_copy(1, j).wait_recv()

        for a in range(anc_row):
            block, found = listed(1, a + 2)
            at = slice(a * width, (a + 1) * width)
            value = base[span(j), at] + dot_t(x1[j], block) * found
            value = value.astype(BF16)
            for cc in range(cols):
                within = a % per_half * width
                packed[cc, j, a // per_half, :, within : within + width] = value[
                    cc * narrow : (cc + 1) * narrow
                ]
            if a % per_half == per_half - 1:
                for d in range(1, cols):
                    y_copy(d, j, a // per_half).start()
        if k == 0:
            low_out[1] = x1[row].astype(F32).T.astype(BF16)

    def z_copy(j, slot, target, h):
        return pltpu.make_async_remote_copy(
            src_ref=z_out.at[j, h],
            dst_ref=z_in.at[slot, h],
            send_sem=z_send.at[j, h],
            recv_sem=z_recv.at[slot, h],
            device_id={"layer": target},
            device_id_type=MESH,
        )

    def merge(j, h):
        for d in range(1, cols):
            y_copy(d, j, h).wait_recv()
        merged = packed[col, j, h].astype(F32)
        for d in range(1, cols):
            merged = merged + y_in[d - 1, j, h].astype(F32)

        @pl.when(jnp.logical_and(j == last, layer == 1))
        def _():
            z_copy(j, layers, layer, h).wait_recv()
            z_out[j, h] = (merged + z_in[layers, h].astype(F32)).astype(BF16)
            z_copy(j, layer, j, h).start()

        @pl.when(jnp.logical_and(j == 0, layer == last - 1))
        def _():
            z_copy(j, layers + 1, layer, h).wait_recv()
            z_out[j, h] = (merged + z_in[layers + 1, h].astype(F32)).astype(BF16)
            z_copy(j, layer, j, h).start()

        @pl.when(jnp.logical_and(j == last, layer == 0))
        def _():
            z_out[j, h] = merged.astype(BF16)
            z_copy(j, layers, 1, h).start()

        @pl.when(jnp.logical_and(j == 0, layer == last))
        def _():
            z_out[j, h] = merged.astype(BF16)
            z_copy(j, layers + 1, last - 1, h).start()

        direct = jnp.logical_and(j != layer, j != relayed)
        direct = jnp.logical_and(direct, jnp.abs(layer - j) != last)

        @pl.when(direct)
        def _():
            z_out[j, h] = merged.astype(BF16)
            z_copy(j, layer, j, h).start()

        @pl.when(j == layer)
        def _():
            z_in[layer, h] = merged.astype(BF16)

    for j in merge_order:
        for h in range(halves):
            merge(j, h)

    loads[6].wait()
    loads[7].wait()
    for s in range(layers):

        @pl.when(jnp.abs(layer - s) == last)
        def _():
            z_in[s] = jnp.zeros_like(z_in[s])

        @pl.when(jnp.logical_and(layer != s, jnp.abs(layer - s) != last))
        def _():
            for h in range(halves):
                z_copy(s, s, layer, h).wait_recv()

    for a in range(anc_row):
        residual = rhs_anc[a].astype(F32)
        for s in range(layers):
            within = a % per_half * width
            piece = z_in[s, a // per_half, :, within : within + width]
            residual = residual - piece.astype(F32)
        anc_out[a] = dot_t(residual.astype(BF16), inv_anc[a])


    @pl.when(active)
    def _():
        for k in range(rows):
            if k == 0:

                @pl.when(goal != col)
                def _():
                    p_copy(0).wait_send()

            else:
                p_copy(k).wait_send()

    for k in range(1, rows):
        x_copy(k, row).wait_send()
    for k in range(rows):
        j = ordered(k)
        for d in range(1, cols):
            for h in range(halves):
                y_copy(d, j, h).wait_send()

        @pl.when(j != layer)
        def _():
            for h in range(halves):
                z_copy(j, layer, j, h).wait_send()


def hand_over(low, anc, low_out, anc_out, sem):
    first = pltpu.make_async_copy(anc, anc_out, sem.at[0])
    second = pltpu.make_async_copy(low, low_out, sem.at[1])
    first.start()
    second.start()
    first.wait()
    second.wait()


def on_device(sizes, rhs_low, inv_low, blocks, targets, rhs_anc, inv_anc):
    layers, rows, cols = sizes
    levels, slots = blocks.shape[3], blocks.shape[4]
    width, cases = rhs_low.shape[3], rhs_low.shape[4]
    anc_row, narrow = rhs_anc.shape[0], rhs_anc.shape[2]
    share = cases // rows
    halves = anc_row
    assert levels == 2 and layers == rows and layers > 3 and cols <= rows and cols * narrow == share
    any_space = pl.BlockSpec(memory_space=pltpu.HBM)
    dma = pltpu.SemaphoreType.DMA
    low, anc = pl.pallas_call(
        functools.partial(kernel, sizes),
        out_shape=(
            pltpu.VMEM((levels, width, share), BF16),
            pltpu.VMEM((anc_row, narrow, width), F32),
        ),
        in_specs=[any_space] * 6,
        out_specs=(pl.BlockSpec(memory_space=pltpu.VMEM), pl.BlockSpec(memory_space=pltpu.VMEM)),
        scratch_shapes=[
            pltpu.VMEM((levels, width, cases), BF16),
            pltpu.VMEM((levels, width, width), BF16),
            pltpu.VMEM((slots, width, width), BF16),
            pltpu.VMEM((slots, width, width), BF16),
            pltpu.VMEM((anc_row, narrow, width), BF16),
            pltpu.VMEM((anc_row, width, width), BF16),
            pltpu.VMEM((cases, width), BF16),
            pltpu.VMEM((rows, share, width), BF16),
            pltpu.VMEM((rows, share, width), BF16),
            pltpu.VMEM((cols, share, width), BF16),
            pltpu.VMEM((share, width), F32),
            pltpu.VMEM((cases, anc_row * width), F32),
            pltpu.VMEM((cols, rows, halves, narrow, anc_row * width // halves), BF16),
            pltpu.VMEM((cols - 1, rows, halves, narrow, anc_row * width // halves), BF16),
            pltpu.VMEM((layers, halves, narrow, anc_row * width // halves), BF16),
            pltpu.VMEM((layers + 2, halves, narrow, anc_row * width // halves), BF16),
            pltpu.SMEM((levels, slots), jnp.int32),
            dma((9,)),
            dma((rows,)),
            dma((cols,)),
            dma((rows,)),
            dma((rows,)),
            dma((cols - 1, rows, halves)),
            dma((cols - 1, rows, halves)),
            dma((layers, halves)),
            dma((layers + 2, halves)),
        ],
        compiler_params=pltpu.CompilerParams(
            collective_id=0, has_side_effects=True, vmem_limit_bytes=56 * 1024 * 1024
        ),
    )(
        targets.reshape(levels, slots),
        rhs_low.reshape(levels, width, cases),
        inv_low.reshape(levels, width, width),
        blocks.reshape(levels, slots, width, width),
        rhs_anc.transpose(0, 2, 1),
        inv_anc,
    )
    low, anc = pl.pallas_call(
        hand_over,
        out_shape=(
            jax.ShapeDtypeStruct(low.shape, low.dtype),
            jax.ShapeDtypeStruct(anc.shape, anc.dtype),
        ),
        in_specs=[pl.BlockSpec(memory_space=pltpu.VMEM)] * 2,
        out_specs=(any_space, any_space),
        scratch_shapes=[dma((2,))],
        compiler_params=pltpu.CompilerParams(vmem_limit_bytes=4 * 1024 * 1024),
    )(low, anc)
    return low[None, :, None], anc.transpose(0, 2, 1)


def solution(mesh):
    sizes = tuple(mesh.shape[a] for a in ("layer", "row", "col"))
    in_specs = (
        P("layer", None, "col", None, None),
        P("layer", None, "col", None, None),
        P("layer", "row", "col", None, None, None, None),
        P("layer", "row", "col", None, None),
        P("row", None, ("layer", "col")),
        P("row", None, None),
    )
    out_specs = (P("layer", None, "col", None, "row"), P("row", None, ("layer", "col")))
    return jax.shard_map(
        functools.partial(on_device, sizes),
        mesh=mesh,
        in_specs=in_specs,
        out_specs=out_specs,
        check_vma=False,
    )
```
